32 devices in a mesh: depth: 2 (over x), tx: 4 (over y, core), ty: 4 (over z).
Axes of the slice: x: 2, y: 2, z: 4, core: 2. Of those that a mesh axis runs over, the one named last changes fastest.
Arguments:
- volume: float32 [32, 1024, 512], P('depth', 'tx', 'ty'), may hold values from -6 to 6
- centers: float32 [4], replicated, may hold values from -1.5 to 1.5
- widths: float32 [4], replicated, may hold values from 0.3 to 1
- density: float32 [4], replicated, may hold values from 0.5 to 6
- colors: float32 [3, 4], replicated, may hold values from 0.05 to 1
Outputs:
- image: float32 [4, 1024, 512], P(None, ('tx', 'depth'), 'ty')
The draws below stay inside these ranges and needn't reach their ends.
All inputs are finite; a program needn't handle non-finite values.
Results may differ from the reference program's by a relative error of at most 0.0001.
Values sent between devices are 32-bit elements; how exact they have to be, the bound alone decides.
No kernel may reach another device: no remote copies, remote signals or barrier semaphores. Data moves between devices by JAX's collectives and lax.ppermute only.
A program may use at most 64 MiB of HBM per device.

```python
import math
import jax
import jax.numpy as jnp
from jax import lax

BUMPS = 4
IMG_X = 1024
IMG_Y = 512
NZ = 32


def block_scale(key, shape, pieces, smallest, high):
    factor_of, own = 1.0, jax.random.fold_in(key, 6)
    for axis_at, shards_of in pieces:
        draws = jnp.exp(jax.random.uniform(jax.random.fold_in(own, axis_at), (shards_of,), jnp.float32, smallest / len(pieces), high / len(pieces)))
        factor_of = factor_of * jnp.repeat(draws, shape[axis_at] // shards_of).reshape([-1 if axis == axis_at else 1 for axis in range(len(shape))])
    return factor_of


def bell_draw(own_key, shape, width, bound, pieces=(), kind=jnp.bfloat16):
    array = jax.random.normal(own_key, shape, jnp.float32) * width
    if len(pieces) > 0:
        array = block_scale(own_key, shape, pieces, -0.22, 0.18) * array
    return jnp.clip(array, min=-bound, max=bound).astype(kind)


def setup_inputs(seed: int = 0) -> dict:
    streams_of = jax.random.split(jax.random.key(seed), 6)
    volume = bell_draw(streams_of[0], (NZ, IMG_X, IMG_Y), 1.0, 6.0, ((0, 2), (1, 4), (2, 4)), jnp.float32)
    centers = jnp.clip(jax.random.uniform(streams_of[1], (BUMPS,), jnp.float32, -1.5, 1.5), -1.5, 1.5)
    widths = jnp.clip(jnp.exp(jax.random.uniform(streams_of[2], (BUMPS,), jnp.float32, math.log(0.3), math.log(1.0))), 0.3, 1.0)
    density = jnp.clip(jnp.exp(jax.random.uniform(streams_of[3], (BUMPS,), jnp.float32, math.log(0.5), math.log(6.0))), 0.5, 6.0)
    colors = jnp.clip(jax.random.uniform(streams_of[4], (3, BUMPS), jnp.float32, 0.05, 1.0), 0.05, 1.0)
    return dict(volume=volume, centers=centers, widths=widths, density=density, colors=colors)


LIGHT_X = 0.36
LIGHT_Y = 0.48
LIGHT_Z = 0.8

def composite(colour, trans, before, current, after, centers, widths, density, colors, step_len):
    middle = current[1:-1, 1:-1]
    grad_x = (current[2:, 1:-1] - current[:-2, 1:-1]) * 0.5
    grad_y = (current[1:-1, 2:] - current[1:-1, :-2]) * 0.5
    grad_z = (after - before) * 0.5
    grad_sq = grad_x * grad_x + grad_y * grad_y + grad_z * grad_z
    facing = jnp.abs(grad_x * LIGHT_X + grad_y * LIGHT_Y + grad_z * LIGHT_Z) * lax.rsqrt(grad_sq + 1.0)
    shade = 0.2 + 0.8 * facing
    scaled = (middle[None] - centers[:, None, None]) / widths[:, None, None]
    bumps = jnp.exp(-scaled * scaled)
    sigma = lax.optimization_barrier(jnp.sum(density[:, None, None] * bumps, 0)) * (1.0 - 0.8 / (1.0 + grad_sq))
    tint = lax.optimization_barrier(jnp.sum(colors[:, :, None, None] * bumps[None], 1))
    shaded = shade[None] * tint / (1.0 + lax.optimization_barrier(jnp.sum(bumps, 0)))[None]
    passed = jnp.exp(-sigma * step_len)
    colour = colour + (trans * (1.0 - passed))[None] * shaded
    trans = trans * passed
    return (colour, trans)

def reference(volume, centers, widths, density, colors):
    depth_total = volume.shape[0]
    step_len = 1.0 / depth_total
    blank = jnp.zeros(volume.shape[1:], volume.dtype)

    def advance(index, state_pair):
        colour, trans = state_pair
        index = jnp.asarray(index).astype(jnp.int32)
        lower = jnp.maximum(index - 1, 0).astype(jnp.int32)
        higher = jnp.minimum(index + 1, depth_total - 1).astype(jnp.int32)
        before = jnp.where(index > 0, lax.dynamic_index_in_dim(volume, lower, 0, keepdims=False), blank)
        after = jnp.where(index < depth_total - 1, lax.dynamic_index_in_dim(volume, higher, 0, keepdims=False), blank)
        current = jnp.pad(lax.dynamic_index_in_dim(volume, index, 0, keepdims=False), 1)
        return composite(colour, trans, before, current, after, centers, widths, density, colors, step_len)
    start = (jnp.zeros((3,) + volume.shape[1:], jnp.float32), jnp.ones(volume.shape[1:], jnp.float32))
    colour, trans = lax.fori_loop(0, depth_total, advance, start)
    return jnp.concatenate([colour, (1.0 - trans)[None]], 0)
```

```python
import functools
import math

import jax
import jax.numpy as jnp
from jax import lax
from jax.experimental import pallas as pl
from jax.experimental.pallas import tpu as pltpu
from jax.sharding import PartitionSpec as P

LIGHT_X = 0.36
LIGHT_Y = 0.48
LIGHT_Z = 0.8
AMBIENT = 0.2
PAD = 8
ROWS_AT_ONCE = 4
FRONT = ("centers", "widths", "density", "colors")

ANY = pl.BlockSpec(memory_space=pl.ANY)
VMEM = pl.BlockSpec(memory_space=pltpu.VMEM)
SMEM = pl.BlockSpec(memory_space=pltpu.SMEM)


def in_vmem(array):
    return pltpu.with_memory_space_constraint(array, pltpu.VMEM)


def vmem_out(*shape):
    return pltpu.VMEM(shape, jnp.float32)


def sends(low, high, even):
    return jnp.where(even, high, low), jnp.where(even, low, high)


def receives(first, second, place, count):
    even = place % 2 == 0
    low = jnp.where(even, second, first)
    high = jnp.where(even, first, second)
    return jnp.where(place > 0, low, 0.0), jnp.where(place < count - 1, high, 0.0)


def swap_rounds(axis, beside=None):
    count = lax.axis_size(axis)
    first = [(i, i ^ 1) for i in range(count)]
    inner = {i: (i + 1 if i % 2 else i - 1) for i in range(1, count - 1)}
    if beside is None or lax.axis_size(beside) % 2:
        second = [(i, inner.get(i, count - 1 - i)) for i in range(count)]
        return (axis, first), (axis, second)
    second = []
    for b in range(lax.axis_size(beside)):
        for i in range(count):
            to = (b, inner[i]) if i in inner else (b ^ 1, i)
            second.append((b * count + i, to[0] * count + to[1]))
    return (axis, first), ((beside, axis), second)


def pack_kernel(volume, padded, cols, col_a, col_b, row_a, row_b, depth_a, depth_b, packed, turned, sems):
    slices, rows, lanes = volume.shape

    def copy(s):
        return pltpu.make_async_copy(
            volume.at[s], padded.at[s, pl.ds(PAD, rows), :], sems.at[s]
        )

    for s in range(slices):
        copy(s).start()
    lane = lax.broadcasted_iota(jnp.int32, (rows, lanes), 1)
    packed[...] = jnp.zeros_like(packed)
    for s in range(slices):
        copy(s).wait()
        moved = pltpu.roll(padded[s, pl.ds(PAD, rows), :], 2 * s + 1, 1)
        packed[...] = jnp.where(lane // 2 == s, moved, packed[...])
    even_y = lax.axis_index("ty") % 2 == 0
    for h in range(rows // lanes):
        turned[h] = packed[pl.ds(h * lanes, lanes), :].T
        last = turned[h, pl.ds(0, slices, 2), :]
        first = turned[h, pl.ds(1, slices, 2), :]
        cols[0, h] = first
        cols[1, h] = last
        col_a[h], col_b[h] = sends(first, last, even_y)
    even_x = lax.axis_index("tx") % 2 == 0
    row_a[...], row_b[...] = sends(padded[:, PAD, :], padded[:, PAD + rows - 1, :], even_x)
    even_z = lax.axis_index("depth") % 2 == 0
    low = padded[0, pl.ds(PAD, rows), :]
    high = padded[slices - 1, pl.ds(PAD, rows), :]
    depth_a[...], depth_b[...] = sends(low, high, even_z)


def render(padded, edges, below, above, consts, outs, first_row, rows, step_len):
    centers, widths, density, colors = consts
    slices, _, lanes = padded.shape
    terms = centers.shape[0]
    tile = (8, lanes)
    log2e = math.log2(math.e)

    def splat(x):
        return jnp.full(tile, x, jnp.float32)

    beta = [splat(-log2e) / (splat(widths[k]) * splat(widths[k])) for k in range(terms)]
    thick = [splat(density[k]) * (-log2e * step_len) for k in range(terms)]
    centre = [splat(centers[k]) for k in range(terms)]
    lane = lax.broadcasted_iota(jnp.int32, tile, 1)
    edge = (lane == 0) | (lane == lanes - 1)
    zero, one = jnp.zeros(tile, jnp.float32), jnp.ones(tile, jnp.float32)

    def chunk(index, _):
        base = pl.multiple_of(first_row + index * (8 * ROWS_AT_ONCE), 8)
        for j in range(ROWS_AT_ONCE):
            row = pl.multiple_of(base + 8 * j, 8)
            edge_rows = edges[pl.ds(row, 8), :]
            total, trans = [zero] * terms, one
            before = below(row)
            current = padded[0, pl.ds(row + PAD, 8), :]
            for s in range(slices):
                after = padded[s + 1, pl.ds(row + PAD, 8), :] if s + 1 < slices else above(row)
                dx = padded[s, pl.ds(row + PAD + 1, 8), :] - padded[s, pl.ds(row + PAD - 1, 8), :]
                dy = pltpu.roll(current, lanes - 1, 1) - pltpu.roll(current, 1, 1)
                dy = dy + jnp.where(edge, pltpu.roll(edge_rows, lanes - (2 * s + 1), 1), 0.0)
                dz = after - before
                bumps = []
                for k in range(terms):
                    off = current - centre[k]
                    bumps.append(jnp.exp2(off * beta[k] * off))
                inv = lax.rsqrt((dx * dx + dy * dy) + (dz * dz + 4.0))
                lit = jnp.abs(dx * (LIGHT_X / LIGHT_Z) + dy * (LIGHT_Y / LIGHT_Z) + dz)
                shade = lit * inv + AMBIENT / ((1 - AMBIENT) * LIGHT_Z)
                extinct = (thick[0] * bumps[0] + thick[1] * bumps[1])
                weight = bumps[0] + bumps[1]
                for k in range(2, terms):
                    extinct = extinct + thick[k] * bumps[k]
                    weight = weight + bumps[k]
                passed = jnp.exp2(extinct * (1.0 - 3.2 * (inv * inv)))
                left = trans * passed
                amount = (trans - left) * (shade / (weight + 1.0))
                total = [total[k] + amount * bumps[k] for k in range(terms)]
                trans = left
                before, current = current, after
            at = pl.multiple_of(row - first_row, 8)
            for c in range(3):
                mixed = total[0] * (colors[c, 0] * ((1 - AMBIENT) * LIGHT_Z))
                for k in range(1, terms):
                    mixed = mixed + total[k] * (colors[c, k] * ((1 - AMBIENT) * LIGHT_Z))
                outs[c, pl.ds(at, 8), :] = mixed
            outs[3, pl.ds(at, 8), :] = trans
        return 0

    lax.fori_loop(0, rows // (8 * ROWS_AT_ONCE), chunk, 0)


def depth_faces(depth_a, depth_b):
    place, count = lax.axis_index("depth"), lax.axis_size("depth")
    even = place % 2 == 0

    def below(row):
        face = jnp.where(even, depth_b[pl.ds(row, 8), :], depth_a[pl.ds(row, 8), :])
        return jnp.where(place > 0, face, 0.0)

    def above(row):
        face = jnp.where(even, depth_a[pl.ds(row, 8), :], depth_b[pl.ds(row, 8), :])
        return jnp.where(place < count - 1, face, 0.0)

    return below, above


def first_kernel(rows_out, start_of, step_len, centers, widths, density, colors, padded, cols, col_a, col_b, row_a, row_b, depth_a, depth_b, full, edges, outs, turned):
    slices, _, lanes = padded.shape
    rows = edges.shape[0]
    left, right = receives(col_a[...], col_b[...], lax.axis_index("ty"), lax.axis_size("ty"))
    turned[...] = jnp.zeros_like(turned)
    for h in range(rows // lanes):
        turned[h, pl.ds(0, slices, 2), :] = right[h] - cols[0, h]
        turned[h, pl.ds(1, slices, 2), :] = cols[1, h] - left[h]
        edges[pl.ds(h * lanes, lanes), :] = turned[h].T
    top, bottom = receives(row_a[...], row_b[...], lax.axis_index("tx"), lax.axis_size("tx"))
    full[:, PAD - 1, :] = top
    full[:, PAD + rows, :] = bottom
    below, above = depth_faces(depth_a, depth_b)
    render(full, edges, below, above, (centers, widths, density, colors), outs, start_of(), rows_out, step_len)


def second_kernel(rows_out, start_of, step_len, centers, widths, density, colors, full, edges, depth_a, depth_b, outs):
    below, above = depth_faces(depth_a, depth_b)
    render(full, edges, below, above, (centers, widths, density, colors), outs, start_of(), rows_out, step_len)


def join_kernel(own, other, image):
    first = lax.axis_index("depth") == 0
    ahead = jnp.where(first, own[3], other[3])
    for c in range(3):
        a, b = own[c], other[c]
        image[c] = jnp.where(first, a, b) + ahead * jnp.where(first, b, a)
    image[3] = 1.0 - own[3] * other[3]


def chain_kernel(parts, image):
    count = parts.shape[0]
    trans = parts[0, 3]
    mix = [parts[0, c] for c in range(3)]
    for d in range(1, count):
        mix = [mix[c] + trans * parts[d, c] for c in range(3)]
        trans = trans * parts[d, 3]
    for c in range(3):
        image[c] = mix[c]
    image[3] = 1.0 - trans


def on_device(volume, centers, widths, density, colors):
    slices, rows, lanes = volume.shape
    depth_count = lax.axis_size("depth")
    part = rows // depth_count
    step_len = 1.0 / (slices * depth_count)
    face = vmem_out(rows, lanes)
    side = (rows // lanes, slices, lanes)
    turned = vmem_out(rows // lanes, lanes, lanes)
    padded, cols, col_a, col_b, row_a, row_b, depth_a, depth_b = pl.pallas_call(
        pack_kernel,
        out_shape=(
            vmem_out(slices, rows + 2 * PAD, lanes),
            vmem_out(2, *side),
            vmem_out(*side),
            vmem_out(*side),
            vmem_out(slices, lanes),
            vmem_out(slices, lanes),
            face,
            face,
        ),
        in_specs=[ANY],
        out_specs=(VMEM,) * 8,
        scratch_shapes=[
            vmem_out(rows, lanes),
            turned,
            pltpu.SemaphoreType.DMA((slices,)),
        ],
        name="pack",
    )(volume)

    depth_rounds = swap_rounds("depth")
    col_rounds = swap_rounds("ty", "tx")
    row_rounds = swap_rounds("tx")

    def send(array, to):
        axes, pairs = to
        return lax.ppermute(array, axes, pairs)

    depth_a = send(depth_a, depth_rounds[0])
    depth_b = send(depth_b, depth_rounds[1]) if depth_count > 2 else depth_a
    col_a = send(col_a, col_rounds[0])
    col_b = send(col_b, col_rounds[1])
    row_a = send(row_a, row_rounds[0])
    row_b = send(row_b, row_rounds[1])
    consts = (centers, widths, density, colors)
    halos = tuple(map(in_vmem, (padded, cols, col_a, col_b, row_a, row_b, depth_a, depth_b)))

    pair = depth_count == 2

    def others_rows():
        return (1 - lax.axis_index("depth")) * part if pair else 0

    def own_rows():
        return lax.axis_index("depth") * part

    sent_rows = part if pair else rows
    full, edges, sent = pl.pallas_call(
        functools.partial(first_kernel, sent_rows, others_rows, step_len),
        out_shape=(
            vmem_out(slices, rows + 2 * PAD, lanes),
            face,
            vmem_out(4, sent_rows, lanes),
        ),
        in_specs=[SMEM] * 4 + [VMEM] * 8,
        out_specs=(VMEM,) * 3,
        scratch_shapes=[turned],
        input_output_aliases={4: 0},
        name="first",
    )(*consts, *halos)
    image = jax.ShapeDtypeStruct((4, part, lanes), jnp.float32)
    if not pair:
        parts = jnp.swapaxes(sent.reshape(4, depth_count, part, lanes), 0, 1)
        parts = lax.all_to_all(parts, "depth", 0, 0)
        return pl.pallas_call(chain_kernel, out_shape=image, name="chain")(parts)
    other = lax.ppermute(sent, "depth", [(0, 1), (1, 0)])
    own = pl.pallas_call(
        functools.partial(second_kernel, part, own_rows, step_len),
        out_shape=vmem_out(4, part, lanes),
        in_specs=[SMEM] * 4 + [VMEM] * 4,
        out_specs=VMEM,
        name="second",
    )(*consts, in_vmem(full), in_vmem(edges), halos[6], halos[7])
    return pl.pallas_call(
        join_kernel,
        out_shape=image,
        in_specs=[VMEM] * 2,
        out_specs=VMEM,
        name="join",
    )(in_vmem(own), in_vmem(other))


def solution(mesh):
    return jax.shard_map(
        on_device,
        mesh=mesh,
        in_specs=(P("depth", "tx", "ty"), P(), P(), P(), P()),
        out_specs=P(None, ("tx", "depth"), "ty"),
        check_vma=False,
    )
```

```python
import functools
import math

import jax
import jax.numpy as jnp
from jax import lax
from jax.experimental import pallas as pl
from jax.experimental.pallas import tpu as pltpu
from jax.sharding import PartitionSpec as P

LIGHT_X = 0.36
LIGHT_Y = 0.48
LIGHT_Z = 0.8
AMBIENT = 0.2
PAD = 8
ROWS_AT_ONCE = 4
LOADS = 4

ANY = pl.BlockSpec(memory_space=pl.ANY)
VMEM = pl.BlockSpec(memory_space=pltpu.VMEM)
ROOM = pltpu.CompilerParams(vmem_limit_bytes=8 << 20)
SMEM = pl.BlockSpec(memory_space=pltpu.SMEM)


def in_vmem(array):
    return pltpu.with_memory_space_constraint(array, pltpu.VMEM)


def in_hbm(array):
    return pltpu.with_memory_space_constraint(array, pltpu.HBM)


def vmem_out(*shape):
    return pltpu.VMEM(shape, jnp.float32)


def sends(low, high, even):
    return jnp.where(even, high, low), jnp.where(even, low, high)


def receives(first, second, place, count):
    even = place % 2 == 0
    low = jnp.where(even, second, first)
    high = jnp.where(even, first, second)
    return jnp.where(place > 0, low, 0.0), jnp.where(place < count - 1, high, 0.0)


def swap_rounds(axis, beside=None):
    count = lax.axis_size(axis)
    first = [(i, i ^ 1) for i in range(count)]
    inner = {i: (i + 1 if i % 2 else i - 1) for i in range(1, count - 1)}
    if beside is None or lax.axis_size(beside) % 2:
        second = [(i, inner.get(i, count - 1 - i)) for i in range(count)]
        return (axis, first), (axis, second)
    second = []
    for b in range(lax.axis_size(beside)):
        for i in range(count):
            to = (b, inner[i]) if i in inner else (b ^ 1, i)
            second.append((b * count + i, to[0] * count + to[1]))
    return (axis, first), ((beside, axis), second)


def pack_kernel(volume, padded, cols, col_a, col_b, row_a, row_b, *rest):
    *depth, packed, turned, sems = rest
    slices, rows, lanes = volume.shape

    group = slices // sems.shape[0]

    def copy(g):
        some = pl.ds(g * group, group)
        return pltpu.make_async_copy(
            volume.at[some], padded.at[some, pl.ds(PAD, rows), :], sems.at[g]
        )

    for g in range(sems.shape[0]):
        copy(g).start()
    lane = lax.broadcasted_iota(jnp.int32, (rows, lanes), 1)
    packed[...] = jnp.zeros_like(packed)
    for s in range(slices):
        if s % group == 0:
            copy(s // group).wait()
        moved = pltpu.roll(padded[s, pl.ds(PAD, rows), :], 2 * s + 1, 1)
        packed[...] = jnp.where(lane // 2 == s, moved, packed[...])
    even_y = lax.axis_index("ty") % 2 == 0
    for h in range(rows // lanes):
        turned[h] = packed[pl.ds(h * lanes, lanes), :].T
        last = turned[h, pl.ds(0, slices, 2), :]
        first = turned[h, pl.ds(1, slices, 2), :]
        cols[0, h] = first
        cols[1, h] = last
        col_a[h], col_b[h] = sends(first, last, even_y)
    even_x = lax.axis_index("tx") % 2 == 0
    row_a[...], row_b[...] = sends(padded[:, PAD, :], padded[:, PAD + rows - 1, :], even_x)
    even_z = lax.axis_index("depth") % 2 == 0
    low = padded[0, pl.ds(PAD, rows), :]
    high = padded[slices - 1, pl.ds(PAD, rows), :]
    faces = sends(low, high, even_z)
    for ref, face in zip(depth, faces):
        ref[...] = face


def constants(consts, tile, step_len):
    centers, widths, density, _ = consts
    log2e = math.log2(math.e)

    def splat(x):
        return jnp.full(tile, x, jnp.float32)

    terms = range(centers.shape[0])
    beta = [splat(-log2e) / (splat(widths[k]) * splat(widths[k])) for k in terms]
    thick = [splat(density[k]) * (-log2e * step_len) for k in terms]
    return [splat(centers[k]) for k in terms], beta, thick


def transfer(current, centre, beta, thick):
    bumps = []
    for k in range(len(beta)):
        off = current - centre[k]
        bumps.append(jnp.exp2(off * beta[k] * off))
    extinct, weight = thick[0] * bumps[0], bumps[0] + 1.0
    for k in range(1, len(beta)):
        extinct = extinct + thick[k] * bumps[k]
        weight = weight + bumps[k]
    return bumps, extinct, weight


def prepare(padded, consts, pre, first_row, step_len):
    count, slices, rows, lanes = pre.shape
    tile = (8, lanes)
    values = constants(consts, tile, step_len)

    def chunk(index, _):
        for j in range(ROWS_AT_ONCE):
            at = pl.multiple_of((index * ROWS_AT_ONCE + j) * 8, 8)
            row = pl.multiple_of(first_row + at, 8)
            for s in range(slices):
                bumps, extinct, weight = transfer(padded[s, pl.ds(row + PAD, 8), :], *values)
                share = 1.0 / weight
                for k in range(count - 1):
                    pre[k, s, pl.ds(at, 8), :] = bumps[k] * share
                pre[count - 1, s, pl.ds(at, 8), :] = extinct
        return 0

    lax.fori_loop(0, rows // (8 * ROWS_AT_ONCE), chunk, 0)


def render(padded, edges, below, above, consts, outs, first_row, step_len, pre=None, pre_row=0):
    colors = consts[3]
    slices, _, lanes = padded.shape
    rows = outs.shape[1]
    terms = colors.shape[1]
    tile = (8, lanes)
    values = constants(consts, tile, step_len) if pre is None else None
    lane = lax.broadcasted_iota(jnp.int32, tile, 1)
    edge = (lane == 0) | (lane == lanes - 1)
    zero, one = jnp.zeros(tile, jnp.float32), jnp.ones(tile, jnp.float32)

    def chunk(index, _):
        for j in range(ROWS_AT_ONCE):
            at = pl.multiple_of((index * ROWS_AT_ONCE + j) * 8, 8)
            row = pl.multiple_of(first_row + at, 8)
            pre_at = pl.multiple_of(pre_row + at, 8)
            edge_rows = edges[pl.ds(row, 8), :]
            total, trans = [zero] * terms, one
            before = below(row)
            current = padded[0, pl.ds(row + PAD, 8), :]
            for s in range(slices):
                after = padded[s + 1, pl.ds(row + PAD, 8), :] if s + 1 < slices else above(row)
                dx = padded[s, pl.ds(row + PAD + 1, 8), :] - padded[s, pl.ds(row + PAD - 1, 8), :]
                dy = pltpu.roll(current, lanes - 1, 1) - pltpu.roll(current, 1, 1)
                dy = dy + jnp.where(edge, pltpu.roll(edge_rows, lanes - (2 * s + 1), 1), 0.0)
                dz = after - before
                inv = lax.rsqrt((dx * dx + dy * dy) + (dz * dz + 4.0))
                lit = jnp.abs(dx * (LIGHT_X / LIGHT_Z) + dy * (LIGHT_Y / LIGHT_Z) + dz)
                shade = lit * inv + AMBIENT / ((1 - AMBIENT) * LIGHT_Z)
                if pre is None:
                    bumps, extinct, weight = transfer(current, *values)
                    shade = shade / weight
                else:
                    bumps = [pre[k, s, pl.ds(pre_at, 8), :] for k in range(terms)]
                    extinct = pre[terms, s, pl.ds(pre_at, 8), :]
                passed = jnp.exp2(extinct * (1.0 - 3.2 * (inv * inv)))
                left = trans * passed
                amount = (trans - left) * shade
                total = [total[k] + amount * bumps[k] for k in range(terms)]
                trans = left
                before, current = current, after
            for c in range(3):
                mixed = total[0] * (colors[c, 0] * ((1 - AMBIENT) * LIGHT_Z))
                for k in range(1, terms):
                    mixed = mixed + total[k] * (colors[c, k] * ((1 - AMBIENT) * LIGHT_Z))
                outs[c, pl.ds(at, 8), :] = mixed
            outs[3, pl.ds(at, 8), :] = trans
        return 0

    lax.fori_loop(0, rows // (8 * ROWS_AT_ONCE), chunk, 0)


def depth_faces(depth_a, depth_b):
    place, count = lax.axis_index("depth"), lax.axis_size("depth")
    even = place % 2 == 0

    def below(row):
        face = jnp.where(even, depth_b[pl.ds(row, 8), :], depth_a[pl.ds(row, 8), :])
        return jnp.where(place > 0, face, 0.0)

    def above(row):
        face = jnp.where(even, depth_a[pl.ds(row, 8), :], depth_b[pl.ds(row, 8), :])
        return jnp.where(place < count - 1, face, 0.0)

    return below, above


def turn_edges(cols, col_a, col_b, edges, turned):
    _, chunks, slices, lanes = cols.shape
    left, right = receives(col_a[...], col_b[...], lax.axis_index("ty"), lax.axis_size("ty"))
    turned[...] = jnp.zeros_like(turned)
    for h in range(chunks):
        turned[h, pl.ds(0, slices, 2), :] = right[h] - cols[0, h]
        turned[h, pl.ds(1, slices, 2), :] = cols[1, h] - left[h]
        edges[pl.ds(h * lanes, lanes), :] = turned[h].T


def fill_rows(row_a, row_b, full):
    top, bottom = receives(row_a[...], row_b[...], lax.axis_index("tx"), lax.axis_size("tx"))
    full[:, PAD - 1, :] = top
    full[:, full.shape[1] - PAD, :] = bottom


def partner_rows(rows, inner):
    ahead = lax.axis_index("depth") == 0
    quarter = rows // 4
    at = jnp.where(ahead == inner, 0, quarter)
    return pl.multiple_of(jnp.where(ahead, 2 * quarter, 0) + at, 8), pl.multiple_of(at, 8)


def before_kernel(step_len, centers, widths, density, colors, padded, pre):
    rows = 2 * pre.shape[2]
    start = pl.multiple_of((1 - lax.axis_index("depth")) * (rows // 2), 8)
    prepare(padded, (centers, widths, density, colors), pre, start, step_len)


def inner_kernel(step_len, centers, widths, density, colors, padded, pre, cols, col_a, col_b, depth_a, edges, outs, turned):
    turn_edges(cols, col_a, col_b, edges, turned)
    below, above = depth_faces(depth_a, depth_a)
    row, pre_row = partner_rows(edges.shape[0], True)
    render(padded, edges, below, above, (centers, widths, density, colors), outs, row, step_len, pre, pre_row)


def outer_kernel(step_len, centers, widths, density, colors, padded, pre, edges, row_a, row_b, depth_a, full, outs):
    fill_rows(row_a, row_b, full)
    below, above = depth_faces(depth_a, depth_a)
    row, pre_row = partner_rows(edges.shape[0], False)
    render(full, edges, below, above, (centers, widths, density, colors), outs, row, step_len, pre, pre_row)


def own_kernel(step_len, centers, widths, density, colors, full, edges, depth_a, outs):
    below, above = depth_faces(depth_a, depth_a)
    row = pl.multiple_of(lax.axis_index("depth") * outs.shape[1], 8)
    render(full, edges, below, above, (centers, widths, density, colors), outs, row, step_len)


def whole_kernel(step_len, centers, widths, density, colors, padded, cols, col_a, col_b, row_a, row_b, depth_a, depth_b, full, outs, edges, turned):
    turn_edges(cols, col_a, col_b, edges, turned)
    fill_rows(row_a, row_b, full)
    below, above = depth_faces(depth_a, depth_b)
    render(full, edges, below, above, (centers, widths, density, colors), outs, 0, step_len)


def join_kernel(own, inner, outer, image):
    ahead = lax.axis_index("depth") == 0
    rows = inner.shape[1]
    for part, at in ((inner, jnp.where(ahead, rows, 0)), (outer, jnp.where(ahead, 0, rows))):
        some = pl.ds(pl.multiple_of(at, 8), rows)
        trans = jnp.where(ahead, own[3, some], part[3])
        for c in range(3):
            a, b = own[c, some], part[c]
            image[c, some] = jnp.where(ahead, a, b) + trans * jnp.where(ahead, b, a)
        image[3, some] = 1.0 - own[3, some] * part[3]


def chain_kernel(parts, image):
    count = parts.shape[0]
    trans = parts[0, 3]
    mix = [parts[0, c] for c in range(3)]
    for d in range(1, count):
        mix = [mix[c] + trans * parts[d, c] for c in range(3)]
        trans = trans * parts[d, 3]
    for c in range(3):
        image[c] = mix[c]
    image[3] = 1.0 - trans


def swap(array, to):
    axes, pairs = to
    return in_vmem(lax.ppermute(array, axes, pairs))


def on_device(volume, centers, widths, density, colors):
    slices, rows, lanes = volume.shape
    depth_count = lax.axis_size("depth")
    pair = depth_count == 2
    part = rows // depth_count
    step_len = 1.0 / (slices * depth_count)
    consts = tuple(map(in_hbm, (centers, widths, density, colors)))
    block = vmem_out(slices, rows + 2 * PAD, lanes)
    face = vmem_out(rows, lanes)
    side = (rows // lanes, slices, lanes)
    turned = vmem_out(rows // lanes, lanes, lanes)
    image = jax.ShapeDtypeStruct((4, part, lanes), jnp.float32)
    out_shape = (block, vmem_out(2, *side)) + (vmem_out(*side),) * 2 + (vmem_out(slices, lanes),) * 2 + (face,) * (1 if pair else 2)
    padded, cols, col_a, col_b, row_a, row_b, *depth = pl.pallas_call(
        pack_kernel,
        out_shape=out_shape,
        in_specs=[ANY],
        out_specs=(VMEM,) * len(out_shape),
        scratch_shapes=[face, turned, pltpu.SemaphoreType.DMA((math.gcd(slices, LOADS),))],
        compiler_params=ROOM,
        name="pack",
    )(in_hbm(volume))
    padded, cols = in_vmem(padded), in_vmem(cols)

    depth = [swap(array, to) for array, to in zip(depth, swap_rounds("depth"))]
    col_a, col_b = (swap(array, to) for array, to in zip((col_a, col_b), swap_rounds("ty", "tx")))
    row_rounds = swap_rounds("tx")
    row_a = swap(row_a, row_rounds[0])
    row_b = swap(row_b, row_rounds[1])

    def call(kernel, out_shape, args, scratch=(), aliases={}):
        return pl.pallas_call(
            functools.partial(kernel, step_len),
            out_shape=out_shape,
            in_specs=[SMEM] * 4 + [VMEM] * len(args),
            out_specs=jax.tree.map(lambda _: VMEM, out_shape),
            scratch_shapes=scratch,
            input_output_aliases=aliases,
            compiler_params=ROOM,
        )(*consts, *args)

    if not pair:
        _, sent = call(
            whole_kernel,
            (block, vmem_out(4, rows, lanes)),
            (padded, cols, col_a, col_b, row_a, row_b, *depth),
            [face, turned],
            {4: 0},
        )
        parts = jnp.swapaxes(sent.reshape(4, depth_count, part, lanes), 0, 1)
        parts = lax.all_to_all(parts, "depth", 0, 0)
        return pl.pallas_call(chain_kernel, out_shape=image, compiler_params=ROOM, name="chain")(parts)

    both = ("depth", [(0, 1), (1, 0)])
    pre = in_vmem(call(before_kernel, vmem_out(colors.shape[1] + 1, slices, part, lanes), (padded,)))
    edges, inner = call(
        inner_kernel, (face, vmem_out(4, part // 2, lanes)), (padded, pre, cols, col_a, col_b, *depth), [turned]
    )
    edges = in_vmem(edges)
    other_inner = swap(inner, both)
    full, outer = call(
        outer_kernel, (block, vmem_out(4, part // 2, lanes)), (padded, pre, edges, row_a, row_b, *depth), aliases={4: 0}
    )
    other_outer = swap(outer, both)
    own = call(own_kernel, vmem_out(4, part, lanes), (in_vmem(full), edges, *depth))
    return pl.pallas_call(
        join_kernel,
        out_shape=image,
        in_specs=[VMEM] * 3,
        out_specs=VMEM,
        compiler_params=ROOM,
        name="join",
    )(in_vmem(own), other_inner, other_outer)


def solution(mesh):
    return jax.shard_map(
        on_device,
        mesh=mesh,
        in_specs=(P("depth", "tx", "ty"), P(), P(), P(), P()),
        out_specs=P(None, ("tx", "depth"), "ty"),
        check_vma=False,
    )
```

```python
import functools
import math

import jax
import jax.numpy as jnp
from jax import lax
from jax.experimental import pallas as pl
from jax.experimental.pallas import tpu as pltpu
from jax.sharding import PartitionSpec as P

LIGHT_X = 0.36
LIGHT_Y = 0.48
LIGHT_Z = 0.8
AMBIENT = 0.2
PAD = 8
ROWS_AT_ONCE = 4
LOADS = 4

ANY = pl.BlockSpec(memory_space=pl.ANY)
VMEM = pl.BlockSpec(memory_space=pltpu.VMEM)
ROOM = pltpu.CompilerParams(vmem_limit_bytes=8 << 20)


def in_vmem(array):
    return pltpu.with_memory_space_constraint(array, pltpu.VMEM)


def in_hbm(array):
    return pltpu.with_memory_space_constraint(array, pltpu.HBM)


def vmem_out(*shape):
    return pltpu.VMEM(shape, jnp.float32)


def sends(low, high, even):
    return jnp.where(even, high, low), jnp.where(even, low, high)


def receives(first, second, place, count):
    even = place % 2 == 0
    low = jnp.where(even, second, first)
    high = jnp.where(even, first, second)
    return jnp.where(place > 0, low, 0.0), jnp.where(place < count - 1, high, 0.0)


def swap_rounds(axis, beside=None):
    count = lax.axis_size(axis)
    first = [(i, i ^ 1) for i in range(count)]
    inner = {i: (i + 1 if i % 2 else i - 1) for i in range(1, count - 1)}
    if beside is None or lax.axis_size(beside) % 2:
        second = [(i, inner.get(i, count - 1 - i)) for i in range(count)]
        return (axis, first), (axis, second)
    second = []
    for b in range(lax.axis_size(beside)):
        for i in range(count):
            to = (b, inner[i]) if i in inner else (b ^ 1, i)
            second.append((b * count + i, to[0] * count + to[1]))
    return (axis, first), ((beside, axis), second)


def pack_kernel(step_len, volume, *rest):
    consts, rest = rest[:4], rest[4:]
    table, padded, cols, col_a, col_b, row_a, row_b, *rest = rest
    *depth, packed, turned = rest[:-6]
    scalars, (sems, const_sems) = rest[-6:-2], rest[-2:]
    slices, rows, lanes = volume.shape

    group = slices // sems.shape[0]

    def copy(g):
        some = pl.ds(g * group, group)
        return pltpu.make_async_copy(
            volume.at[some], padded.at[some, pl.ds(PAD, rows), :], sems.at[g]
        )

    for g in range(sems.shape[0]):
        copy(g).start()
    loads = [pltpu.make_async_copy(*each) for each in zip(consts, scalars, [const_sems.at[i] for i in range(4)])]
    for load in loads:
        load.start()
    for load in loads:
        load.wait()
    fill_table(scalars, table, step_len)
    lane = lax.broadcasted_iota(jnp.int32, (rows, lanes), 1)
    packed[...] = jnp.zeros_like(packed)
    for s in range(slices):
        if s % group == 0:
            copy(s // group).wait()
        moved = pltpu.roll(padded[s, pl.ds(PAD, rows), :], 2 * s + 1, 1)
        packed[...] = jnp.where(lane // 2 == s, moved, packed[...])
    even_y = lax.axis_index("ty") % 2 == 0
    for h in range(rows // lanes):
        turned[h] = packed[pl.ds(h * lanes, lanes), :].T
        last = turned[h, pl.ds(0, slices, 2), :]
        first = turned[h, pl.ds(1, slices, 2), :]
        cols[0, h] = first
        cols[1, h] = last
        col_a[h], col_b[h] = sends(first, last, even_y)
    even_x = lax.axis_index("tx") % 2 == 0
    row_a[...], row_b[...] = sends(padded[:, PAD, :], padded[:, PAD + rows - 1, :], even_x)
    even_z = lax.axis_index("depth") % 2 == 0
    low = padded[0, pl.ds(PAD, rows), :]
    high = padded[slices - 1, pl.ds(PAD, rows), :]
    faces = sends(low, high, even_z)
    for ref, face in zip(depth, faces):
        ref[...] = face


def fill_table(scalars, table, step_len):
    centers, widths, density, colors = scalars
    tile = table.shape[1:]
    terms = centers.shape[0]

    def splat(x):
        return jnp.full(tile, x, jnp.float32)

    for k in range(terms):
        table[k] = splat(centers[k])
        table[terms + k] = splat(-math.log2(math.e)) / (splat(widths[k]) * splat(widths[k]))
        if k == 0:
            table[2 * terms] = splat(density[0]) * (-math.log2(math.e) * step_len)
        else:
            table[2 * terms + k] = splat(density[k]) / splat(density[0])
        for c in range(3):
            table[(3 + c) * terms + k] = splat(colors[c, k]) * ((1 - AMBIENT) * LIGHT_Z)


def transfer(current, table):
    terms = table.shape[0] // 6
    bumps = []
    for k in range(terms):
        off = current - table[k]
        bumps.append(jnp.exp2(off * table[terms + k] * off))
    extinct, weight = bumps[0], bumps[0] + 1.0
    for k in range(1, terms):
        extinct = extinct + table[2 * terms + k] * bumps[k]
        weight = weight + bumps[k]
    return bumps, extinct, weight


def prepare(padded, table, pre, first_row):
    count, slices, rows, _ = pre.shape

    def chunk(index, _):
        for j in range(ROWS_AT_ONCE):
            at = pl.multiple_of((index * ROWS_AT_ONCE + j) * 8, 8)
            row = pl.multiple_of(first_row + at, 8)
            for s in range(slices):
                bumps, extinct, weight = transfer(padded[s, pl.ds(row + PAD, 8), :], table)
                share = 1.0 / weight
                for k in range(count - 1):
                    pre[k, s, pl.ds(at, 8), :] = bumps[k] * share
                pre[count - 1, s, pl.ds(at, 8), :] = extinct
        return 0

    lax.fori_loop(0, rows // (8 * ROWS_AT_ONCE), chunk, 0)


def render(padded, edges, below, above, table, outs, first_row, pre=None):
    slices, _, lanes = padded.shape
    rows = outs.shape[1]
    terms = table.shape[0] // 6
    tile = (8, lanes)
    thick = table[2 * terms]
    thick_lit = thick * 3.2
    lane = lax.broadcasted_iota(jnp.int32, tile, 1)
    edge = (lane == 0) | (lane == lanes - 1)
    zero, one = jnp.zeros(tile, jnp.float32), jnp.ones(tile, jnp.float32)

    def chunk(index, _):
        for j in range(ROWS_AT_ONCE):
            at = pl.multiple_of((index * ROWS_AT_ONCE + j) * 8, 8)
            row = pl.multiple_of(first_row + at, 8)
            edge_rows = edges[pl.ds(row, 8), :]
            total, trans = [zero] * terms, one
            before = below(row)
            current = padded[0, pl.ds(row + PAD, 8), :]
            for s in range(slices):
                after = padded[s + 1, pl.ds(row + PAD, 8), :] if s + 1 < slices else above(row)
                dx = padded[s, pl.ds(row + PAD + 1, 8), :] - padded[s, pl.ds(row + PAD - 1, 8), :]
                dy = pltpu.roll(current, lanes - 1, 1) - pltpu.roll(current, 1, 1)
                dy = dy + jnp.where(edge, pltpu.roll(edge_rows, lanes - (2 * s + 1), 1), 0.0)
                dz = after - before
                inv = lax.rsqrt((dx * dx + dy * dy) + (dz * dz + 4.0))
                lit = jnp.abs(dx * (LIGHT_X / LIGHT_Z) + dy * (LIGHT_Y / LIGHT_Z) + dz)
                shade = lit * inv + AMBIENT / ((1 - AMBIENT) * LIGHT_Z)
                if pre is None:
                    bumps, extinct, weight = transfer(current, table)
                    shade = shade / weight
                else:
                    bumps = [pre[k, s, pl.ds(at, 8), :] for k in range(terms)]
                    extinct = pre[terms, s, pl.ds(at, 8), :]
                passed = jnp.exp2(extinct * (thick - thick_lit * (inv * inv)))
                left = trans * passed
                amount = (trans - left) * shade
                total = [total[k] + amount * bumps[k] for k in range(terms)]
                trans = left
                before, current = current, after
            for c in range(3):
                mixed = total[0] * table[(3 + c) * terms]
                for k in range(1, terms):
                    mixed = mixed + total[k] * table[(3 + c) * terms + k]
                outs[c, pl.ds(at, 8), :] = mixed
            outs[3, pl.ds(at, 8), :] = trans
        return 0

    lax.fori_loop(0, rows // (8 * ROWS_AT_ONCE), chunk, 0)


def depth_faces(depth_a, depth_b):
    place, count = lax.axis_index("depth"), lax.axis_size("depth")
    even = place % 2 == 0

    def below(row):
        face = jnp.where(even, depth_b[pl.ds(row, 8), :], depth_a[pl.ds(row, 8), :])
        return jnp.where(place > 0, face, 0.0)

    def above(row):
        face = jnp.where(even, depth_a[pl.ds(row, 8), :], depth_b[pl.ds(row, 8), :])
        return jnp.where(place < count - 1, face, 0.0)

    return below, above


def turn_edges(cols, col_a, col_b, edges, turned):
    _, chunks, slices, lanes = cols.shape
    left, right = receives(col_a[...], col_b[...], lax.axis_index("ty"), lax.axis_size("ty"))
    turned[...] = jnp.zeros_like(turned)
    for h in range(chunks):
        turned[h, pl.ds(0, slices, 2), :] = right[h] - cols[0, h]
        turned[h, pl.ds(1, slices, 2), :] = cols[1, h] - left[h]
        edges[pl.ds(h * lanes, lanes), :] = turned[h].T


def fill_rows(row_a, row_b, full):
    top, bottom = receives(row_a[...], row_b[...], lax.axis_index("tx"), lax.axis_size("tx"))
    full[:, PAD - 1, :] = top
    full[:, full.shape[1] - PAD, :] = bottom


def partner_rows(rows, inner):
    ahead = lax.axis_index("depth") == 0
    quarter = rows // 4
    return pl.multiple_of(jnp.where(ahead, 2 * quarter, 0) + jnp.where(ahead == inner, 0, quarter), 8)


def before_kernel(table, padded, pre):
    rows = 4 * pre.shape[2]
    prepare(padded, table, pre, partner_rows(rows, True))


def inner_kernel(table, padded, pre, cols, col_a, col_b, depth_a, edges, outs, turned):
    turn_edges(cols, col_a, col_b, edges, turned)
    below, above = depth_faces(depth_a, depth_a)
    render(padded, edges, below, above, table, outs, partner_rows(edges.shape[0], True), pre)


def outer_kernel(table, padded, edges, row_a, row_b, depth_a, full, outs):
    fill_rows(row_a, row_b, full)
    below, above = depth_faces(depth_a, depth_a)
    render(full, edges, below, above, table, outs, partner_rows(edges.shape[0], False))


def own_kernel(table, full, edges, depth_a, outs):
    below, above = depth_faces(depth_a, depth_a)
    row = pl.multiple_of(lax.axis_index("depth") * outs.shape[1], 8)
    render(full, edges, below, above, table, outs, row)


def whole_kernel(table, padded, cols, col_a, col_b, row_a, row_b, depth_a, depth_b, full, outs, edges, turned):
    turn_edges(cols, col_a, col_b, edges, turned)
    fill_rows(row_a, row_b, full)
    below, above = depth_faces(depth_a, depth_b)
    render(full, edges, below, above, table, outs, 0)


def join_kernel(own, inner, outer, image):
    ahead = lax.axis_index("depth") == 0
    rows = inner.shape[1]
    for part, at in ((inner, jnp.where(ahead, rows, 0)), (outer, jnp.where(ahead, 0, rows))):
        some = pl.ds(pl.multiple_of(at, 8), rows)
        trans = jnp.where(ahead, own[3, some], part[3])
        for c in range(3):
            a, b = own[c, some], part[c]
            image[c, some] = jnp.where(ahead, a, b) + trans * jnp.where(ahead, b, a)
        image[3, some] = 1.0 - own[3, some] * part[3]


def chain_kernel(parts, image):
    count = parts.shape[0]
    trans = parts[0, 3]
    mix = [parts[0, c] for c in range(3)]
    for d in range(1, count):
        mix = [mix[c] + trans * parts[d, c] for c in range(3)]
        trans = trans * parts[d, 3]
    for c in range(3):
        image[c] = mix[c]
    image[3] = 1.0 - trans


def swap(array, to):
    axes, pairs = to
    return in_vmem(lax.ppermute(array, axes, pairs))


def on_device(volume, centers, widths, density, colors):
    slices, rows, lanes = volume.shape
    depth_count = lax.axis_size("depth")
    pair = depth_count == 2
    part = rows // depth_count
    step_len = 1.0 / (slices * depth_count)
    consts = tuple(map(in_hbm, (centers, widths, density, colors)))
    block = vmem_out(slices, rows + 2 * PAD, lanes)
    face = vmem_out(rows, lanes)
    side = (rows // lanes, slices, lanes)
    turned = vmem_out(rows // lanes, lanes, lanes)
    image = jax.ShapeDtypeStruct((4, part, lanes), jnp.float32)
    terms = centers.shape[0]
    out_shape = (vmem_out(6 * terms, 8, lanes), block, vmem_out(2, *side)) + (vmem_out(*side),) * 2 + (vmem_out(slices, lanes),) * 2 + (face,) * (1 if pair else 2)
    table, padded, cols, col_a, col_b, row_a, row_b, *depth = pl.pallas_call(
        functools.partial(pack_kernel, step_len),
        out_shape=out_shape,
        in_specs=[ANY] * 5,
        out_specs=(VMEM,) * len(out_shape),
        scratch_shapes=[face, turned]
        + [pltpu.SMEM(each.shape, jnp.float32) for each in consts]
        + [pltpu.SemaphoreType.DMA((math.gcd(slices, LOADS),)), pltpu.SemaphoreType.DMA((4,))],
        compiler_params=ROOM,
        name="pack",
    )(in_hbm(volume), *consts)
    table, padded, cols = in_vmem(table), in_vmem(padded), in_vmem(cols)

    depth = [swap(array, to) for array, to in zip(depth, swap_rounds("depth"))]
    col_a, col_b = (swap(array, to) for array, to in zip((col_a, col_b), swap_rounds("ty", "tx")))
    row_rounds = swap_rounds("tx")
    row_a = swap(row_a, row_rounds[0])
    row_b = swap(row_b, row_rounds[1])

    def call(kernel, out_shape, args, scratch=(), aliases={}):
        return pl.pallas_call(
            kernel,
            out_shape=out_shape,
            in_specs=[VMEM] * (1 + len(args)),
            out_specs=jax.tree.map(lambda _: VMEM, out_shape),
            scratch_shapes=scratch,
            input_output_aliases=aliases,
            compiler_params=ROOM,
        )(table, *args)

    if not pair:
        _, sent = call(
            whole_kernel,
            (block, vmem_out(4, rows, lanes)),
            (padded, cols, col_a, col_b, row_a, row_b, *depth),
            [face, turned],
            {1: 0},
        )
        parts = jnp.swapaxes(sent.reshape(4, depth_count, part, lanes), 0, 1)
        parts = lax.all_to_all(parts, "depth", 0, 0)
        return pl.pallas_call(chain_kernel, out_shape=image, compiler_params=ROOM, name="chain")(parts)

    both = ("depth", [(0, 1), (1, 0)])
    pre = in_vmem(call(before_kernel, vmem_out(terms + 1, slices, part // 2, lanes), (padded,)))
    edges, inner = call(
        inner_kernel, (face, vmem_out(4, part // 2, lanes)), (padded, pre, cols, col_a, col_b, *depth), [turned]
    )
    edges = in_vmem(edges)
    other_inner = swap(inner, both)
    full, outer = call(
        outer_kernel, (block, vmem_out(4, part // 2, lanes)), (padded, edges, row_a, row_b, *depth), aliases={1: 0}
    )
    other_outer = swap(outer, both)
    own = call(own_kernel, vmem_out(4, part, lanes), (in_vmem(full), edges, *depth))
    return pl.pallas_call(
        join_kernel,
        out_shape=image,
        in_specs=[VMEM] * 3,
        out_specs=VMEM,
        compiler_params=ROOM,
        name="join",
    )(in_vmem(own), other_inner, other_outer)


def solution(mesh):
    return jax.shard_map(
        on_device,
        mesh=mesh,
        in_specs=(P("depth", "tx", "ty"), P(), P(), P(), P()),
        out_specs=P(None, ("tx", "depth"), "ty"),
        check_vma=False,
    )
```
